32 devices in a mesh: dp: 8 (over z, x), fsdp: 4 (over y, core).
Axes of the slice: x: 2, y: 2, z: 4, core: 2. Of those that a mesh axis runs over, the one named last changes fastest.
Arguments:
- tokens: int32 [2, 32, 256], P(None, ('dp', 'fsdp')), may hold values from 0 to 32
- targets: int32 [2, 32, 256], P(None, ('dp', 'fsdp')), may hold values from 0 to 32
- lengths: int32 [2, 32], P(None, ('dp', 'fsdp')), may hold values from 64 to 256, as said below
- loss_mask: int32 [2, 32, 256], P(None, ('dp', 'fsdp')), may hold values from 0 to 1
- in_proj: float32 [2, 480, 3840], P(None, None, ('dp', 'fsdp'))
- in_bias: float32 [2, 3840], P(None, ('dp', 'fsdp')), may hold values from -1.75 to 1.75
- out_proj: float32 [3840, 480], P(('dp', 'fsdp')), may hold values from -0.125 to 0.125
- vectors: float32 [12, 480], replicated, may hold values from -0.5 to 1.3
- embedding: float32 [33, 480], replicated, may hold values from -0.625 to 0.625
- in_rows: float32 [2, 5, 480], replicated, may hold values from 4e-06 to 8e-05
- in_cols: float32 [2, 3840], P(None, ('dp', 'fsdp')), may hold values from 4e-06 to 8e-05
- out_rows: float32 [3840], P(('dp', 'fsdp')), may hold values from 4e-06 to 8e-05
- out_cols: float32 [2, 480], replicated, may hold values from 4e-06 to 8e-05
- bias_moment: float32 [2, 3840], P(None, ('dp', 'fsdp')), may hold values from 0.004 to 0.02
- vector_moment: float32 [12, 480], replicated, may hold values from 4e-06 to 8e-05
- embed_rows: float32 [33], replicated, may hold values from 4e-06 to 8e-05
- embed_cols: float32 [480], replicated, may hold values from 4e-06 to 8e-05
Outputs:
- loss: float32 [], replicated
- new_in_proj: float32 [2, 480, 3840], P(None, None, ('dp', 'fsdp'))
- new_in_bias: float32 [2, 3840], P(None, ('dp', 'fsdp'))
- new_out_proj: float32 [3840, 480], P(('dp', 'fsdp'))
- new_vectors: float32 [12, 480], replicated
- new_embedding: float32 [33, 480], replicated
- new_in_rows: float32 [2, 5, 480], replicated
- new_in_cols: float32 [2, 3840], P(None, ('dp', 'fsdp'))
- new_out_rows: float32 [3840], P(('dp', 'fsdp'))
- new_out_cols: float32 [2, 480], replicated
- new_bias_moment: float32 [2, 3840], P(None, ('dp', 'fsdp'))
- new_vector_moment: float32 [12, 480], replicated
- new_embed_rows: float32 [33], replicated
- new_embed_cols: float32 [480], replicated
The draws below stay inside these ranges and needn't reach their ends.
Inputs may be any that keep to these rules, and one draw needn't show every extreme that they name: Positions from lengths on are padding: never attended to and never scored.
All inputs are finite; a program needn't handle non-finite values.
Results may differ from the reference program's by a relative error of at most 0.0013.
The reference program's roundings to bfloat16 on the way count: a program that leaves them out, or rounds other values in their place, can miss the bound.
Values may be sent and summed in bfloat16 or wider, within the bound.
No kernel may reach another device: no remote copies, remote signals or barrier semaphores. Data moves between devices by JAX's collectives and lax.ppermute only.
A program may use at most 192 MiB of HBM per device.

```python
import math
import jax
import jax.numpy as jnp
from jax import lax

MODEL_WIDTH = 480
HEADS = 20
HEAD_DIM = 24
FF = 1920
VOCAB = 33
LAYERS = 2
MICRO = 2
SEQ_LEN = 256
SEQS = 32
COLS = 3840
VECS = 12


def draw_lengths(key, part):
    shortest_len = SEQ_LEN // 4
    drawn = jax.random.randint(jax.random.fold_in(key, 1), (MICRO, SEQS), shortest_len, SEQ_LEN + 1, dtype=jnp.int32)
    longest_at = jax.random.randint(jax.random.fold_in(key, 2), (MICRO, 1), 0, SEQS, dtype=jnp.int32)
    shortest_at = jax.random.randint(jax.random.fold_in(key, 3), (MICRO, 1), 0, SEQS, dtype=jnp.int32)
    column = jnp.arange(SEQS, dtype=jnp.int32)[None, :]
    drawn = jnp.where(column == shortest_at, shortest_len, drawn)
    return jnp.where(column == longest_at, SEQ_LEN, drawn)


def draw_loss_mask(key, part):
    sequence = jnp.arange(SEQS, dtype=jnp.int32)
    threshold = 80 + 160 * sequence // SEQS
    ticket = jax.random.randint(key, (MICRO, SEQS, SEQ_LEN), 0, 1000, dtype=jnp.int32)
    return (ticket < threshold[None, :, None]).astype(jnp.int32)


def draw_in_proj(key, part):
    drawn = jax.random.normal(key, (LAYERS, MODEL_WIDTH, 4 * MODEL_WIDTH + FF), jnp.float32)
    column = jnp.arange(4 * MODEL_WIDTH + FF)
    factor = jnp.where((column >= 3 * MODEL_WIDTH) & (column < 4 * MODEL_WIDTH), 6.0, 1.0) / math.sqrt(MODEL_WIDTH)
    return drawn * factor[None, None, :]


def draw_vectors(key, part):
    total_rows = 5 * LAYERS + 2
    row_index = jnp.arange(total_rows)
    within = row_index % 5
    is_gain = jnp.where(row_index < 5 * LAYERS, (within == 0) | (within == 2), row_index == 5 * LAYERS)
    gains = jax.random.uniform(jax.random.fold_in(key, 1), (total_rows, MODEL_WIDTH), jnp.float32, 0.7, 1.3)
    shifts = jax.random.uniform(jax.random.fold_in(key, 2), (total_rows, MODEL_WIDTH), jnp.float32, -0.5, 0.5)
    return jnp.where(is_gain[:, None], gains, shifts)


def set_ends(entries, key, least, top_value):
    shape = entries.shape
    place = [jax.random.randint(jax.random.fold_in(key, axis), (), 0, shape[axis]) for axis in range(len(shape))]
    entries = entries.at[tuple(place)].set(least)
    longest = shape.index(max(shape))
    place[longest] = (place[longest] + 1) % shape[longest]
    return entries.at[tuple(place)].set(top_value)


def steps_of(key, dims, cuts, smallest, top_value):
    level, own = 1.0, jax.random.fold_in(key, 6)
    for dim, shards_of in cuts:
        steps = jnp.exp(jax.random.uniform(jax.random.fold_in(own, dim), (shards_of,), jnp.float32, smallest / len(cuts), top_value / len(cuts)))
        level = level * jnp.repeat(steps, dims[dim] // shards_of).reshape([-1 if axis == dim else 1 for axis in range(len(dims))])
    return level


def bell_draw(rng, dims, scale, reach, split=(), held_as=jnp.bfloat16):
    values = scale * jax.random.normal(rng, dims, jnp.float32)
    if split:
        values = values * steps_of(rng, dims, split, -0.22, 0.18)
    return jnp.clip(values, -reach, reach).astype(held_as)


def setup_inputs(seed: int = 0) -> dict:
    seeds = jax.random.split(jax.random.key(seed), 18)
    return {
        "tokens": set_ends(jax.random.randint(seeds[0], (MICRO, SEQS, SEQ_LEN), 0, VOCAB), jax.random.fold_in(seeds[0], 1), 0, VOCAB - 1).astype(jnp.int32),
        "targets": set_ends(jax.random.randint(seeds[1], (MICRO, SEQS, SEQ_LEN), 0, VOCAB), jax.random.fold_in(seeds[1], 1), 0, VOCAB - 1).astype(jnp.int32),
        "lengths": draw_lengths(jax.random.fold_in(seeds[17], 71), 0),
        "loss_mask": draw_loss_mask(jax.random.fold_in(seeds[17], 71), 0),
        "in_proj": draw_in_proj(jax.random.fold_in(seeds[17], 71), 0),
        "in_bias": bell_draw(seeds[5], (LAYERS, COLS), 0.3, 1.75, ((1, 32),), jnp.float32),
        "out_proj": bell_draw(seeds[6], (LAYERS * FF, MODEL_WIDTH), FF ** -0.5, 0.125, ((0, 32),), jnp.float32),
        "vectors": draw_vectors(jax.random.fold_in(seeds[17], 71), 0),
        "embedding": bell_draw(seeds[8], (VOCAB, MODEL_WIDTH), 0.1, 0.625, (), jnp.float32),
        "in_rows": jnp.clip(jnp.exp(jax.random.uniform(seeds[9], (LAYERS, 5, MODEL_WIDTH), jnp.float32, math.log(3.999999989900971e-06), math.log(7.999999797903001e-05))), 3.999999989900971e-06, 7.999999797903001e-05),
        "in_cols": jnp.clip(jnp.exp(math.log(7.999999797903001e-05) - 2.9957323 * jax.random.uniform(seeds[10], (LAYERS, COLS), jnp.float32) ** steps_of(seeds[10], (LAYERS, COLS), ((1, 32),), -0.2, 0.2)), 3.999999989900971e-06, 7.999999797903001e-05),
        "out_rows": jnp.clip(jnp.exp(math.log(7.999999797903001e-05) - 2.9957323 * jax.random.uniform(seeds[11], (LAYERS * FF,), jnp.float32) ** steps_of(seeds[11], (LAYERS * FF,), ((0, 32),), -0.2, 0.2)), 3.999999989900971e-06, 7.999999797903001e-05),
        "out_cols": jnp.clip(jnp.exp(jax.random.uniform(seeds[12], (LAYERS, MODEL_WIDTH), jnp.float32, math.log(3.999999989900971e-06), math.log(7.999999797903001e-05))), 3.999999989900971e-06, 7.999999797903001e-05),
        "bias_moment": jnp.clip(jnp.exp(math.log(0.02) - 1.6094378 * jax.random.uniform(seeds[13], (LAYERS, COLS), jnp.float32) ** steps_of(seeds[13], (LAYERS, COLS), ((1, 32),), -0.2, 0.2)), 0.004, 0.02),
        "vector_moment": jnp.clip(jnp.exp(jax.random.uniform(seeds[14], (VECS, MODEL_WIDTH), jnp.float32, math.log(3.999999989900971e-06), math.log(7.999999797903001e-05))), 3.999999989900971e-06, 7.999999797903001e-05),
        "embed_rows": jnp.clip(jnp.exp(jax.random.uniform(seeds[15], (VOCAB,), jnp.float32, math.log(3.999999989900971e-06), math.log(7.999999797903001e-05))), 3.999999989900971e-06, 7.999999797903001e-05),
        "embed_cols": jnp.clip(jnp.exp(jax.random.uniform(seeds[16], (MODEL_WIDTH,), jnp.float32, math.log(3.999999989900971e-06), math.log(7.999999797903001e-05))), 3.999999989900971e-06, 7.999999797903001e-05),
    }


EPS_NORM = 1e-05
DECAY = 0.5
CLIP = 0.25
RATE = 0.4
NEGATIVE = -1e+30
FULL_PRECISION = lax.Precision.HIGHEST

@jax.custom_vjp
def reduced_value(v):
    return lax.optimization_barrier(v.astype(jnp.bfloat16)).astype(jnp.float32)

@jax.custom_vjp
def reduced_backward(v):
    return v

def low_keep(v):
    return (reduced_value(v), None)

def low_pass(kept, grad):
    return (grad,)

def back_keep(v):
    return (v, None)

def back_low(kept, grad):
    return (reduced_value(grad),)
reduced_value.defvjp(low_keep, low_pass)
reduced_backward.defvjp(back_keep, back_low)

def norm_rows(values, gain, bias_vector_row):
    center = values - lax.optimization_barrier(jnp.mean(values, axis=-1, keepdims=True))
    spread = lax.optimization_barrier(jnp.mean(center * center, axis=-1, keepdims=True))
    return center * lax.rsqrt(spread + EPS_NORM) * gain + bias_vector_row

def rotary_tables(length, head_size):
    half_size = head_size // 2
    frequency = 10000.0 ** (-(jnp.arange(half_size, dtype=jnp.float32) * 2.0 / head_size))
    angles = jnp.arange(length, dtype=jnp.float32)[:, None] * frequency[None, :]
    angles = jnp.concatenate([angles, angles], axis=-1)
    return (jnp.cos(angles), jnp.sin(angles))

def rotate(values, cosine_table, sine_table):
    half_size = values.shape[-1] // 2
    turned = jnp.concatenate([-values[..., half_size:], values[..., :half_size]], axis=-1)
    return values * cosine_table[:, None, :] + turned * sine_table[:, None, :]

def group_loss(params, tokens, targets, visible, weight, true_count):
    in_proj, in_bias, out_proj, vectors, embedding = params
    sequences, length = tokens.shape
    cosine_table, sine_table = rotary_tables(length, HEAD_DIM)
    score_scale = HEAD_DIM ** (-0.5)
    residual_state = embedding[tokens]
    for layer_index in range(LAYERS):
        starting_row = 5 * layer_index
        weight_matrix = reduced_value(in_proj[layer_index])
        bias_vector_row = reduced_value(in_bias[layer_index])
        second_weight = reduced_value(out_proj[layer_index * FF:(layer_index + 1) * FF])
        normalized_rows = reduced_value(norm_rows(residual_state, vectors[starting_row], vectors[starting_row + 1]))
        projection_output = reduced_backward(jnp.einsum('mrn,nu->mru', normalized_rows, weight_matrix[:, :3 * MODEL_WIDTH], precision=FULL_PRECISION) + bias_vector_row[:3 * MODEL_WIDTH])
        divided = projection_output.reshape(sequences, length, 3, HEADS, HEAD_DIM)
        queries = reduced_value(rotate(divided[:, :, 0], cosine_table, sine_table))
        keys_rot = reduced_value(rotate(divided[:, :, 1], cosine_table, sine_table))
        values = reduced_value(divided[:, :, 2])
        scores = reduced_backward(jnp.einsum('sqhe,skhe->shqk', queries, keys_rot, precision=FULL_PRECISION) * score_scale)
        scores = jnp.where(visible[:, None, None, :], scores, NEGATIVE)
        attend = reduced_value(jax.nn.softmax(scores, axis=-1))
        attention_output = jnp.einsum('shqk,skhe->sqhe', attend, values, precision=FULL_PRECISION).reshape(sequences, length, MODEL_WIDTH)
        attention_output = reduced_backward(reduced_value(attention_output))
        residual_state = residual_state + reduced_backward(jnp.einsum('mrn,nu->mru', attention_output, weight_matrix[:, 3 * MODEL_WIDTH:4 * MODEL_WIDTH], precision=FULL_PRECISION) + bias_vector_row[3 * MODEL_WIDTH:4 * MODEL_WIDTH])
        normalized_rows = reduced_value(norm_rows(residual_state, vectors[starting_row + 2], vectors[starting_row + 3]))
        before_activation = reduced_backward(jnp.einsum('mrn,nu->mru', normalized_rows, weight_matrix[:, 4 * MODEL_WIDTH:], precision=FULL_PRECISION) + bias_vector_row[4 * MODEL_WIDTH:])
        activation_output = reduced_value(jax.nn.gelu(before_activation, approximate=False))
        residual_state = residual_state + reduced_backward(jnp.einsum('enq,qf->enf', activation_output, second_weight, precision=FULL_PRECISION) + vectors[starting_row + 4])
    last_row = 5 * LAYERS
    head_input = reduced_value(norm_rows(residual_state, vectors[last_row], vectors[last_row + 1]))
    vocab_scores = reduced_backward(jnp.einsum('iko,xo->ikx', head_input, reduced_value(embedding), precision=FULL_PRECISION))
    target_hot = (targets[..., None] == jnp.arange(VOCAB, dtype=jnp.int32)).astype(jnp.float32)
    picked = lax.optimization_barrier(jnp.sum(vocab_scores * target_hot, axis=-1))
    return jnp.sum(weight * (jax.scipy.special.logsumexp(vocab_scores, axis=-1) - picked)) / true_count

def shrink(step_now, weight_now):
    rms_step = jnp.sqrt(jnp.mean(step_now * step_now))
    rms_weight = jnp.sqrt(jnp.mean(weight_now * weight_now))
    return RATE * rms_weight * step_now / jnp.maximum(1.0, rms_step / CLIP)

def factored(grad_now, weight_now, rows_old, cols_old):
    square = grad_now * grad_now
    rows_new = DECAY * rows_old + (1.0 - DECAY) * lax.optimization_barrier(jnp.mean(square, axis=1))
    cols_new = DECAY * cols_old + (1.0 - DECAY) * lax.optimization_barrier(jnp.mean(square, axis=0))
    factor_scale = rows_new[:, None] * cols_new[None, :] / jnp.mean(rows_new)
    step_now = grad_now * lax.rsqrt(factor_scale)
    return (weight_now - shrink(step_now, weight_now), rows_new, cols_new)

def plain(grad_now, weight_now, moment_old):
    moment_new = DECAY * moment_old + (1.0 - DECAY) * grad_now * grad_now
    step_now = grad_now * lax.rsqrt(moment_new)
    return (weight_now - shrink(step_now, weight_now), moment_new)

def reference(tokens, targets, lengths, loss_mask, in_proj, in_bias, out_proj, vectors, embedding, in_rows, in_cols, out_rows, out_cols, bias_moment, vector_moment, embed_rows, embed_cols):
    position = jnp.arange(SEQ_LEN, dtype=jnp.int32)
    visible = position[None, None, :] < lengths[:, :, None]
    weight = (loss_mask * visible.astype(jnp.int32)).astype(jnp.float32)
    true_count = jnp.sum(weight)
    group_size = 16

    def regroup(array):
        return array.reshape((-1, group_size) + array.shape[2:])
    batches = (regroup(tokens), regroup(targets), regroup(visible), regroup(weight))
    params = (in_proj, in_bias, out_proj, vectors, embedding)

    def accumulate(carry, group_batch):
        grad_sum, loss_sum = carry

        def objective(weights_now):
            return group_loss(weights_now, group_batch[0], group_batch[1], group_batch[2], group_batch[3], true_count)
        group_value, pullback = jax.vjp(objective, params)
        grad_now, = pullback(jnp.ones_like(group_value))
        return ((jax.tree.map(jnp.add, grad_sum, grad_now), loss_sum + group_value), None)
    initial = (jax.tree.map(jnp.zeros_like, params), jnp.zeros((), jnp.float32))
    (grads, loss), _ = lax.scan(accumulate, initial, batches)
    grad_in, grad_bias, grad_out, grad_vec, embedding_table_gradient = grads
    bounds = [(0, MODEL_WIDTH), (MODEL_WIDTH, 2 * MODEL_WIDTH), (2 * MODEL_WIDTH, 3 * MODEL_WIDTH), (3 * MODEL_WIDTH, 4 * MODEL_WIDTH), (4 * MODEL_WIDTH, 4 * MODEL_WIDTH + FF)]
    proj_layers, rows_layers, cols_layers, bias_layers, moment_layers = ([], [], [], [], [])
    for layer_index in range(LAYERS):
        proj_parts, rows_parts, cols_parts, bias_parts, moment_parts = ([], [], [], [], [])
        for segment_id in range(5):
            first_col, last_col = bounds[segment_id]
            new_block, rows_new, cols_new = factored(grad_in[layer_index, :, first_col:last_col], in_proj[layer_index, :, first_col:last_col], in_rows[layer_index, segment_id], in_cols[layer_index, first_col:last_col])
            proj_parts.append(new_block)
            rows_parts.append(rows_new)
            cols_parts.append(cols_new)
            new_piece, moment_new = plain(grad_bias[layer_index, first_col:last_col], in_bias[layer_index, first_col:last_col], bias_moment[layer_index, first_col:last_col])
            bias_parts.append(new_piece)
            moment_parts.append(moment_new)
        proj_layers.append(jnp.concatenate(proj_parts, axis=1))
        rows_layers.append(jnp.stack(rows_parts))
        cols_layers.append(jnp.concatenate(cols_parts))
        bias_layers.append(jnp.concatenate(bias_parts))
        moment_layers.append(jnp.concatenate(moment_parts))
    new_in_proj = jnp.stack(proj_layers)
    new_in_rows = jnp.stack(rows_layers)
    new_in_cols = jnp.stack(cols_layers)
    new_in_bias = jnp.stack(bias_layers)
    new_bias_moment = jnp.stack(moment_layers)
    out_parts, out_rows_parts, out_cols_parts = ([], [], [])
    for layer_index in range(LAYERS):
        first_row = layer_index * FF
        last_row = first_row + FF
        new_block, rows_new, cols_new = factored(grad_out[first_row:last_row], out_proj[first_row:last_row], out_rows[first_row:last_row], out_cols[layer_index])
        out_parts.append(new_block)
        out_rows_parts.append(rows_new)
        out_cols_parts.append(cols_new)
    new_out_proj = jnp.concatenate(out_parts, axis=0)
    new_out_rows = jnp.concatenate(out_rows_parts)
    new_out_cols = jnp.stack(out_cols_parts)
    new_vector_moment = DECAY * vector_moment + (1.0 - DECAY) * grad_vec * grad_vec
    vector_step = grad_vec * lax.rsqrt(new_vector_moment)
    rms_step = jnp.sqrt(lax.optimization_barrier(jnp.mean(vector_step * vector_step, axis=1, keepdims=True)))
    rms_weight = jnp.sqrt(lax.optimization_barrier(jnp.mean(vectors * vectors, axis=1, keepdims=True)))
    new_vectors = vectors - RATE * rms_weight * vector_step / jnp.maximum(1.0, rms_step / CLIP)
    new_embedding, new_embed_rows, new_embed_cols = factored(embedding_table_gradient, embedding, embed_rows, embed_cols)
    return (loss, new_in_proj, new_in_bias, new_out_proj, new_vectors, new_embedding, new_in_rows, new_in_cols, new_out_rows, new_out_cols, new_bias_moment, new_vector_moment, new_embed_rows, new_embed_cols)
```

```python
import functools

import jax
import jax.numpy as jnp
from jax import lax
from jax.experimental import pallas as pl
from jax.experimental.pallas import tpu as pltpu
from jax.sharding import PartitionSpec as P

HEADS = 20
HEAD_DIM = 24
FF = 1920
LANES = 128

EPS_NORM = 1e-05
DECAY = 0.5
CLIP = 0.25
RATE = 0.4
NEGATIVE = -1e30
AXES = ("dp", "fsdp")
CHUNK = 240

f32 = jnp.float32
bf16 = jnp.bfloat16


def dot(a, b, ca, cb):
    return lax.dot_general(a, b, (((ca,), (cb,)), ((), ())), preferred_element_type=f32)


def dot_nn(a, b):
    return dot(a, b, 1, 0)


def dot_nt(a, b):
    return dot(a, b, 1, 1)


def dot_tn(a, b):
    return dot(a, b, 0, 0)


def normalize(x):
    center = x - jnp.mean(x, axis=0, keepdims=True)
    scale = lax.rsqrt(jnp.mean(center * center, axis=0, keepdims=True) + EPS_NORM)
    return center * scale, scale


def normalize_pull(dh, xh, scale, gain):
    t = dh * gain
    dx = scale * (
        t - jnp.mean(t, axis=0, keepdims=True) - xh * jnp.mean(t * xh, axis=0, keepdims=True)
    )
    return (
        dx,
        jnp.sum(dh * xh, axis=1, keepdims=True),
        jnp.sum(dh, axis=1, keepdims=True),
    )


def extend(a, lanes):
    rows, tokens = a.shape
    tail = (lax.broadcasted_iota(jnp.int32, (lanes - rows, tokens), 0) == 0).astype(bf16)
    return jnp.concatenate([a, tail], axis=0)


def turn(w, cosine, signed_sine):
    return w * cosine + pltpu.roll(w, w.shape[0] // 2, 0) * signed_sine


def turn_back(w, cosine, signed_sine):
    return w * cosine + pltpu.roll(w * signed_sine, w.shape[0] // 2, 0)


def gelu_and_slope(u):
    phi = 0.5 * (1.0 + lax.erf(u * (0.5**0.5)))
    slope = phi + u * (jnp.exp(-0.5 * u * u) * (0.5 / jnp.pi) ** 0.5)
    return u * phi, slope


def split3(v):
    a = v.astype(bf16)
    rest = v - a.astype(f32)
    b = rest.astype(bf16)
    c = (rest - b.astype(f32)).astype(bf16)
    return a, b, c


def attention_forward_kernel(
    first,
    lengths,
    x_in,
    tokens,
    w,
    columns,
    cosine,
    sine,
    x_out,
    q_out,
    k_out,
    v_out,
    peak_out,
    inv_out,
    a_out,
    att_out,
    mid_out,
    qkv,
    att,
):
    features = x_out.shape[0]
    total = x_out.shape[1]
    lanes = w.shape[1]
    length = cosine.shape[1]
    if first:
        table = x_in[...]
        rows = table.shape[1]
        vocab = 33
        index = lax.broadcasted_iota(jnp.int32, (rows, total), 0)
        hot = (index == tokens[...]) & (index < vocab)
        hot = hot.astype(f32).astype(bf16)
        a, b, c = split3(table)
        x = dot_nn(a, hot) + dot_nn(b, hot) + dot_nn(c, hot)
        x_out[...] = x
    else:
        x = x_in[...]
    xh, _ = normalize(x)
    a1 = extend((xh * columns[:, 0:1] + columns[:, 1:2]).astype(bf16), lanes)
    a_out[...] = a1
    qkv[...] = dot_nn(w[0 : 3 * features, :], a1)
    scale = HEAD_DIM ** (-0.5)
    cos = cosine[...]
    sin = sine[...]
    key = lax.broadcasted_iota(jnp.int32, (length, 1), 0)

    def head(h, carry):
        row = pl.multiple_of(h * HEAD_DIM, 8)
        for s in range(total // length):
            here = slice(s * length, (s + 1) * length)
            q = turn(qkv[pl.ds(row, HEAD_DIM), here], cos, sin).astype(bf16)
            k = turn(qkv[pl.ds(row + features, HEAD_DIM), here], cos, sin).astype(bf16)
            v = qkv[pl.ds(row + 2 * features, HEAD_DIM), here].astype(bf16)
            scores = dot_tn(k, q) * scale
            scores = jnp.where(key < lengths[s], scores, NEGATIVE)
            peak = jnp.max(scores, axis=0, keepdims=True)
            raised = jnp.exp(scores - peak)
            inverse = 1.0 / jnp.sum(raised, axis=0, keepdims=True)
            probs = (raised * inverse).astype(bf16)
            att[pl.ds(row, HEAD_DIM), here] = dot_nn(v, probs)
            q_out[h, :, here] = q
            k_out[h, :, here] = k
            v_out[h, :, here] = v
            peak_out[h, :, here] = peak
            inv_out[h, :, here] = inverse
        return carry

    lax.fori_loop(0, HEADS, head, 0)
    attended = extend(att[...].astype(bf16), lanes)
    att_out[...] = attended
    mid_out[...] = x + dot_nn(w[3 * features : 4 * features, :], attended)


def mlp_forward_kernel(x_in, up, down, columns, x_out, a_out, act_out, slope_out):
    features = x_in.shape[0]
    lanes = up.shape[1]
    hidden = up.shape[0]
    x = x_in[...]
    xh, _ = normalize(x)
    a2 = extend((xh * columns[:, 0:1] + columns[:, 1:2]).astype(bf16), lanes)
    a_out[...] = a2
    x_out[...] = x + columns[:, 2:3]

    def chunk(c, carry):
        rows = pl.ds(pl.multiple_of(c * CHUNK, CHUNK), CHUNK)
        act, slope = gelu_and_slope(dot_nn(up[rows, :], a2))
        act = act.astype(bf16)
        act_out[rows, :] = act
        slope_out[rows, :] = slope
        x_out[...] += dot_tn(down[rows, :], act)[0:features]
        return carry

    lax.fori_loop(0, hidden // CHUNK, chunk, 0)


def mlp_backward(dx, x, a2, act, slope, up, down, columns, dup, ddown, bias, vec, back, side):
    features, total = dx.shape
    lanes = up.shape[1]
    hidden = up.shape[0]
    dy = dx.astype(bf16)
    dy_rows = dy.T
    a2_rows = a2[...].T
    back[...] = jnp.zeros_like(back)

    def chunk(c, carry):
        rows = pl.ds(pl.multiple_of(c * CHUNK, CHUNK), CHUNK)
        du = (dot_nn(down[rows, 0:features], dy) * slope[rows, :]).astype(bf16)
        ddown[rows, :] = dot_nn(act[rows, :], dy_rows).astype(ddown.dtype)
        grad = dot_nn(du, a2_rows)
        dup[rows, :] = grad[:, 0:features].astype(dup.dtype)
        side[rows, :] = grad[:, lanes - LANES : lanes]
        back[...] += dot_tn(up[rows, :], du)
        return carry

    lax.fori_loop(0, hidden // CHUNK, chunk, 0)
    spare = features - (lanes - LANES)
    bias[...] = side[...].T[spare : spare + 1, :]
    xh, scale = normalize(x)
    d, dgain, dshift = normalize_pull(back[0:features, :], xh, scale, columns[:, 0:1])
    vec[:, 0:1] = dgain
    vec[:, 1:2] = dshift
    vec[:, 2:3] = jnp.sum(dy.astype(f32), axis=1, keepdims=True)
    return dx + d


def top_kernel(
    inverse,
    x_in,
    up,
    down,
    columns,
    final,
    table,
    targets,
    weight,
    dx_out,
    dup,
    ddown,
    bias,
    vec,
    vec_final,
    table_out,
    loss,
    x_top,
    a_low,
    act,
    slope,
    back,
    side,
):
    features = x_in.shape[0]
    mlp_forward_kernel(x_in, up, down, columns, x_top, a_low, act, slope)
    xh, scale = normalize(x_top[...])
    head = (xh * final[:, 0:1] + final[:, 1:2]).astype(bf16)
    vocab = 33
    low = table[...].astype(bf16)
    logits = dot_nn(low, head)
    row = lax.broadcasted_iota(jnp.int32, logits.shape, 0)
    logits = jnp.where(row < vocab, logits, NEGATIVE)
    hot = row == targets[...]
    peak = jnp.max(logits, axis=0, keepdims=True)
    raised = jnp.exp(logits - peak)
    total = jnp.sum(raised, axis=0, keepdims=True)
    picked = jnp.sum(jnp.where(hot, logits, 0.0), axis=0, keepdims=True)
    w = weight[...]
    loss[...] = jnp.broadcast_to(
        jnp.sum(w * (peak + jnp.log(total) - picked), axis=1, keepdims=True), loss.shape
    )
    dlogits = ((raised / total - hot.astype(f32)) * (w * inverse[0])).astype(bf16)
    table_out[...] = dot_nt(dlogits, head)
    dx, dgain, dshift = normalize_pull(dot_tn(low, dlogits), xh, scale, final[:, 0:1])
    vec_final[:, 0:1] = dgain
    vec_final[:, 1:2] = dshift
    dx_out[...] = mlp_backward(
        dx, x_in[...], a_low, act, slope, up, down, columns, dup, ddown, bias, vec, back, side
    )


def mlp_backward_kernel(
    dx_in, x_in, a2, act, slope, up, down, columns, dx_out, dup, ddown, bias, vec, back, side
):
    dx_out[...] = mlp_backward(
        dx_in[...], x_in[...], a2, act, slope, up, down, columns, dup, ddown, bias, vec, back, side
    )


def attention_backward_kernel(
    first,
    lengths,
    dx_in,
    x_in,
    q_in,
    k_in,
    v_in,
    peak_in,
    inv_in,
    a1,
    attended,
    w,
    columns,
    cosine,
    sine,
    tokens,
    dx_out,
    dw,
    bias,
    vec,
    datt,
    dqkv,
    side,
):
    features, total = dx_in.shape
    lanes = w.shape[1]
    length = cosine.shape[1]
    spare = features - (lanes - LANES)
    scale = HEAD_DIM ** (-0.5)
    cos = cosine[...]
    sin = sine[...]
    dx = dx_in[...]
    dz = dx.astype(bf16)
    grad = dot_nt(dz, attended[...])
    dw[3 * features : 4 * features, :] = grad[:, 0:features].astype(dw.dtype)
    side[3 * features : 4 * features, :] = grad[:, lanes - LANES : lanes]
    datt[...] = dot_tn(w[3 * features : 4 * features, :], dz)[0:features]
    key = lax.broadcasted_iota(jnp.int32, (length, 1), 0)

    def head(h, carry):
        row = pl.multiple_of(h * HEAD_DIM, 8)
        for s in range(total // length):
            here = slice(s * length, (s + 1) * length)
            q = q_in[h, :, here]
            k = k_in[h, :, here]
            v = v_in[h, :, here]
            da = datt[pl.ds(row, HEAD_DIM), here].astype(bf16)
            scores = dot_tn(k, q) * scale
            scores = jnp.where(key < lengths[s], scores, NEGATIVE)
            probs = jnp.exp(scores - peak_in[h, :, here]) * inv_in[h, :, here]
            dprobs = dot_tn(v, da)
            dots = jnp.sum(probs * dprobs, axis=0, keepdims=True)
            dscores = (probs * (dprobs - dots)).astype(bf16)
            dv = dot_nt(da, probs.astype(bf16))
            dk = dot_nt(q, dscores) * scale
            dq = dot_nn(k, dscores) * scale
            dqkv[pl.ds(row, HEAD_DIM), here] = turn_back(dq, cos, sin)
            dqkv[pl.ds(row + features, HEAD_DIM), here] = turn_back(dk, cos, sin)
            dqkv[pl.ds(row + 2 * features, HEAD_DIM), here] = dv
        return carry

    lax.fori_loop(0, HEADS, head, 0)
    low = dqkv[...].astype(bf16)
    grad = dot_nt(low, a1[...])
    dw[0 : 3 * features, :] = grad[:, 0:features].astype(dw.dtype)
    side[0 : 3 * features, :] = grad[:, lanes - LANES : lanes]
    bias[...] = side[...].T[spare : spare + 1, :]
    back = dot_tn(w[0 : 3 * features, :], low)[0:features]
    xh, norm_scale = normalize(x_in[...])
    d, dgain, dshift = normalize_pull(back, xh, norm_scale, columns[:, 0:1])
    vec[:, 0:1] = dgain
    vec[:, 1:2] = dshift
    dx = dx + d
    if first:
        rows = dx_out.shape[0]
        hot = lax.broadcasted_iota(jnp.int32, (rows, total), 0) == tokens[...]
        hot = hot.astype(f32).astype(bf16)
        a, b, c = split3(dx)
        dx_out[...] = dot_nt(hot, a) + dot_nt(hot, b) + dot_nt(hot, c)
    else:
        dx_out[...] = dx


def shape(dims, dtype=f32):
    return jax.ShapeDtypeStruct(dims, dtype)


VM = pl.BlockSpec(memory_space=pltpu.VMEM)
SM = pl.BlockSpec(memory_space=pltpu.SMEM)
PARAMS = pltpu.CompilerParams(vmem_limit_bytes=60 * 2**20)


def call(kernel, scalars, arrays, out, scratch, name):
    return pl.pallas_call(
        kernel,
        out_shape=out,
        in_specs=[SM] * len(scalars) + [VM] * len(arrays),
        out_specs=[VM] * len(out),
        scratch_shapes=[pltpu.VMEM(s.shape, s.dtype) for s in scratch],
        compiler_params=PARAMS,
        name=name,
    )(*scalars, *arrays)


def attention_forward(first, lengths, x, tokens, w, columns, cosine, sine, features, total):
    lanes = w.shape[1]
    out = [
        shape((features, total)) if first else shape((8, LANES)),
        shape((HEADS, HEAD_DIM, total), bf16),
        shape((HEADS, HEAD_DIM, total), bf16),
        shape((HEADS, HEAD_DIM, total), bf16),
        shape((HEADS, 1, total)),
        shape((HEADS, 1, total)),
        shape((lanes, total), bf16),
        shape((lanes, total), bf16),
        shape((features, total)),
    ]
    scratch = [shape((3 * features, total)), shape((features, total))]

    def kernel(lengths, x_in, tokens, w, columns, cosine, sine, x_out, *rest):
        if not first:
            x_out[...] = jnp.zeros_like(x_out)
        attention_forward_kernel(
            first, lengths, x_in, tokens, w, columns, cosine, sine, x_out if first else x_in, *rest
        )

    got = call(
        kernel, [lengths], [x, tokens, w, columns, cosine, sine], out, scratch, "attention_forward"
    )
    if not first:
        got = [x, *got[1:]]
    return got


def mlp_forward(x, up, down, columns):
    features, total = x.shape
    hidden, lanes = up.shape
    out = [
        shape((features, total)),
        shape((lanes, total), bf16),
        shape((hidden, total), bf16),
        shape((hidden, total)),
    ]
    return call(mlp_forward_kernel, [], [x, up, down, columns], out, [], "mlp_forward")


def top(inverse, x, up, down, columns, final, table, targets, weight, dtype):
    features, total = x.shape
    hidden, lanes = up.shape
    out = [
        shape((features, total)),
        shape((hidden, features), dtype),
        shape((hidden, features), dtype),
        shape((1, hidden)),
        shape((features, 8)),
        shape((features, 8)),
        shape(table.shape),
        shape((8, LANES)),
    ]
    scratch = [
        shape((features, total)),
        shape((lanes, total), bf16),
        shape((hidden, total), bf16),
        shape((hidden, total)),
        shape((lanes, total)),
        shape((hidden, LANES)),
    ]
    return call(
        top_kernel,
        [inverse],
        [x, up, down, columns, final, table, targets, weight],
        out,
        scratch,
        "top",
    )


def mlp_back(dx, x, a2, act, slope, up, down, columns, dtype):
    features, total = x.shape
    hidden, lanes = up.shape
    out = [
        shape((features, total)),
        shape((hidden, features), dtype),
        shape((hidden, features), dtype),
        shape((1, hidden)),
        shape((features, 8)),
    ]
    scratch = [shape((lanes, total)), shape((hidden, LANES))]
    return call(
        mlp_backward_kernel,
        [],
        [dx, x, a2, act, slope, up, down, columns],
        out,
        scratch,
        "mlp_backward",
    )


def attention_back(first, lengths, dx, x, saved, w, columns, cosine, sine, tokens, rows, dtype):
    features, total = x.shape
    out = [
        shape((rows, features)) if first else shape((features, total)),
        shape((4 * features, features), dtype),
        shape((1, 4 * features)),
        shape((features, 8)),
    ]
    scratch = [
        shape((features, total)),
        shape((3 * features, total)),
        shape((4 * features, LANES)),
    ]
    return call(
        functools.partial(attention_backward_kernel, first),
        [lengths],
        [dx, x, *saved, w, columns, cosine, sine, tokens],
        out,
        scratch,
        "attention_backward",
    )


def rotary_tables(length):
    half = HEAD_DIM // 2
    frequency = 10000.0 ** (-(jnp.arange(half, dtype=f32) * 2.0 / HEAD_DIM))
    angles = frequency[:, None] * jnp.arange(length, dtype=f32)[None, :]
    cosine = jnp.cos(angles)
    sine = jnp.sin(angles)
    return jnp.concatenate([cosine, cosine], axis=0), jnp.concatenate([-sine, sine], axis=0)


def gradients(w_in, w_out, vectors, embedding, tokens, targets, lengths, weight, inverse, dtype):
    layers = len(w_in)
    features = vectors.shape[1]
    lanes = w_in[0].shape[1]
    vocab = embedding.shape[0]
    total = tokens.size
    length = tokens.shape[-1]
    rows = -(-vocab // 8) * 8
    tokens = tokens.reshape(1, total)
    targets = targets.reshape(1, total)
    weight = weight.reshape(1, total)
    columns = vectors.T
    pick = lambda *r: jnp.stack([columns[:, i] for i in r] + [columns[:, 0]] * (8 - len(r)), axis=1)
    cosine, sine = rotary_tables(length)
    table = jnp.pad(embedding, ((0, rows - vocab), (0, 0)))
    x = jnp.pad(embedding, ((0, LANES - vocab), (0, 0))).T
    saved = []
    for l in range(layers):
        r = 5 * l
        got = attention_forward(
            l == 0,
            lengths,
            x,
            tokens,
            w_in[l][: 4 * features],
            pick(r, r + 1),
            cosine,
            sine,
            features,
            total,
        )
        x, middle = got[0], got[-1]
        entry = {"x": x, "attention": got[1:-1], "middle": middle}
        if l < layers - 1:
            x, a2, act, slope = mlp_forward(
                middle, w_in[l][4 * features :], w_out[l], pick(r + 2, r + 3, r + 4)
            )
            entry["mlp"] = (a2, act, slope)
        saved.append(entry)
    last = 5 * layers
    grads = {}
    vec = [None] * (last + 2)
    for l in reversed(range(layers)):
        r = 5 * l
        entry = saved[l]
        up, down = w_in[l][4 * features :], w_out[l]
        column = pick(r + 2, r + 3, r + 4)
        if l == layers - 1:
            dx, dup, ddown, bias_up, v, vf, table_grad, loss = top(
                inverse,
                entry["middle"],
                up,
                down,
                column,
                pick(last, last + 1),
                table,
                targets,
                weight,
                dtype,
            )
            vec[last], vec[last + 1] = vf[:, 0], vf[:, 1]
        else:
            dx, dup, ddown, bias_up, v = mlp_back(
                dx, entry["middle"], *entry["mlp"], up, down, column, dtype
            )
        vec[r + 2], vec[r + 3], vec[r + 4] = v[:, 0], v[:, 1], v[:, 2]
        dx, dw, bias, v = attention_back(
            l == 0,
            lengths,
            dx,
            entry["x"],
            entry["attention"],
            w_in[l][: 4 * features],
            pick(r, r + 1),
            cosine,
            sine,
            tokens,
            rows,
            dtype,
        )
        vec[r], vec[r + 1] = v[:, 0], v[:, 1]
        grads[l] = (dw, dup, ddown, jnp.concatenate([bias, bias_up], axis=1))
    return grads, jnp.stack(vec), (table_grad + dx)[:vocab], loss[0, 0]


def exchange(array, bit, count):
    return lax.ppermute(array, AXES, [(i, i ^ (1 << bit)) for i in range(count)])


def routes(bits):
    middle = list(range(1, bits - 1))
    turns = [c * len(middle) // 3 for c in range(3)]
    return [middle[t:] + middle[:t] for t in turns]


def gather_rows(shards, slot, count):
    bits = count.bit_length() - 1
    own = [(slot >> b) & 1 for b in range(bits)]

    def join(mine, bit):
        other = exchange(mine, bit, count)
        axis = mine.ndim - 3 - bit
        return jnp.where(
            own[bit] == 0,
            jnp.concatenate([mine, other], axis=axis),
            jnp.concatenate([other, mine], axis=axis),
        )

    rows, lanes = shards[0].shape
    packed = join(jnp.stack(shards).reshape((len(shards),) + (1,) * bits + (rows, lanes)), bits - 1)
    out = []
    for index, order in enumerate(routes(bits)):
        part = packed[index]
        for bit in reversed(order):
            part = join(part, bit)
        out.append(join(part, 0).reshape(count * rows, lanes))
    return out


def scatter_sum(parts, slot, count):
    bits = count.bit_length() - 1
    own = [(slot >> b) & 1 for b in range(bits)]

    def fold(array, bit):
        axis = array.ndim - 3 - bit
        away = lax.dynamic_index_in_dim(array, 1 - own[bit], axis, keepdims=True)
        kept = lax.dynamic_index_in_dim(array, own[bit], axis, keepdims=True)
        return kept.astype(f32) + exchange(away.astype(bf16), bit, count).astype(f32)

    halves = []
    for part, order in zip(parts, routes(bits)):
        rows, lanes = part.shape[0] // count, part.shape[1]
        part = fold(part.reshape((2,) * bits + (rows, lanes)), 0)
        for bit in order:
            part = fold(part, bit)
        halves.append(part)
    total = fold(jnp.stack(halves), bits - 1)
    return [total[i].reshape(rows, lanes) for i in range(len(parts))]


def sum_all(array, count):
    for bit in range(count.bit_length() - 1):
        array = array + exchange(array, bit, count)
    return array


def shrink_factor(step_squares, weight_squares, entries):
    rms_step = jnp.sqrt(step_squares / entries)
    rms_weight = jnp.sqrt(weight_squares / entries)
    return RATE * rms_weight / jnp.maximum(1.0, rms_step / CLIP)


def local(
    count,
    tokens,
    targets,
    lengths,
    loss_mask,
    in_proj,
    in_bias,
    out_proj,
    vectors,
    embedding,
    in_rows,
    in_cols,
    out_rows,
    out_cols,
    bias_moment,
    vector_moment,
    embed_rows,
    embed_cols,
):
    layers, features, part = in_proj.shape
    length = tokens.shape[-1]
    vocab = embedding.shape[0]
    lanes = -(-(features + 3) // LANES) * LANES
    slot = lax.axis_index(AXES)
    position = jnp.arange(length, dtype=jnp.int32)
    visible = position[None, None, :] < lengths[:, :, None]
    weight = (loss_mask * visible.astype(jnp.int32)).astype(f32)
    scored = jnp.sum(loss_mask * visible.astype(jnp.int32))

    w_own = jnp.swapaxes(in_proj, 1, 2)
    extra = jnp.zeros((part, lanes - features - 1), bf16)
    counts = jnp.stack([scored // 256, scored % 256]).astype(bf16)
    shards = []
    for l in range(layers):
        tail = extra.at[0, 0:2].set(counts) if l == 0 else extra
        shards.append(
            jnp.concatenate([w_own[l].astype(bf16), in_bias[l].astype(bf16)[:, None], tail], axis=1)
        )
    shards.append(jnp.pad(out_proj.astype(bf16), ((0, 0), (0, lanes - features))))
    *w_in, w_out = gather_rows(shards, slot, count)
    tallies = w_in[0].reshape(count, part, lanes)[:, 0, features + 1 : features + 3].astype(f32)
    tallies = jnp.sum(tallies, axis=0)
    true_count = tallies[0] * 256.0 + tallies[1]
    inverse = (1.0 / true_count).reshape(1)
    hidden = w_out.shape[0] // layers
    grads, grad_vec, grad_table, loss = gradients(
        w_in,
        [w_out[l * hidden : (l + 1) * hidden] for l in range(layers)],
        vectors,
        embedding,
        tokens,
        targets,
        lengths.reshape(-1),
        weight,
        inverse,
        bf16,
    )
    grad_in = [jnp.concatenate(grads[l][0:2], axis=0) for l in range(layers)]
    grad_out = jnp.concatenate([grads[l][2] for l in range(layers)], axis=0)
    *grad_in, grad_out = scatter_sum([*grad_in, grad_out], slot, count)
    grad_in = jnp.stack(grad_in)
    small = jnp.concatenate(
        [
            grad_vec,
            grad_table,
            jnp.concatenate([grads[l][3] for l in range(layers)], axis=0).reshape(-1, features),
            jnp.full((1, features), loss),
        ],
        axis=0,
    )
    small = sum_all(small, count)
    edges = [vectors.shape[0], vectors.shape[0] + vocab]
    grad_vec, grad_table = small[: edges[0]], small[edges[0] : edges[1]]
    loss = small[-1, 0] / true_count
    grad_bias = lax.dynamic_slice_in_dim(
        small[edges[1] : -1].reshape(layers, -1), slot * part, part, axis=1
    )

    segment = jnp.minimum(slot * part // features, 4)
    here = (jnp.arange(5, dtype=jnp.int32) == segment).astype(f32)
    sizes = jnp.array([features] * 4 + [FF], f32)
    layer_here = (jnp.arange(layers, dtype=jnp.int32) == slot * part // hidden).astype(f32)

    square = grad_in * grad_in
    new_in_cols = DECAY * in_cols + (1.0 - DECAY) * jnp.mean(square, axis=2)
    row_part = jnp.sum(square, axis=1)
    row_step = jnp.sum(square / new_in_cols[:, :, None], axis=1)
    new_bias_moment = DECAY * bias_moment + (1.0 - DECAY) * grad_bias * grad_bias
    bias_step = grad_bias * lax.rsqrt(new_bias_moment)
    square_out = grad_out * grad_out
    new_out_rows = DECAY * out_rows + (1.0 - DECAY) * jnp.mean(square_out, axis=1)
    col_part = jnp.sum(square_out, axis=0)
    col_step = jnp.sum(square_out / new_out_rows[:, None], axis=0)
    per_segment = jnp.stack(
        [
            jnp.sum(in_proj * in_proj, axis=(1, 2)),
            jnp.sum(bias_step * bias_step, axis=1),
            jnp.sum(in_bias * in_bias, axis=1),
        ]
    )
    numbers = jnp.concatenate(
        [
            (per_segment[:, :, None] * here).reshape(-1),
            layer_here * jnp.sum(new_out_rows),
            layer_here * jnp.sum(out_proj * out_proj),
        ]
    )
    stats = jnp.concatenate(
        [
            (row_part[:, None, :] * here[None, :, None]).reshape(-1, features),
            (row_step[:, None, :] * here[None, :, None]).reshape(-1, features),
            layer_here[:, None] * col_part[None, :],
            layer_here[:, None] * col_step[None, :],
            jnp.pad(numbers, (0, features - numbers.shape[0]))[None, :],
        ],
        axis=0,
    )
    stats = sum_all(stats, count)
    k = 5 * layers
    row_sum = stats[0:k].reshape(layers, 5, features)
    row_step = stats[k : 2 * k].reshape(layers, 5, features)
    col_sum = stats[2 * k : 2 * k + layers]
    col_step = stats[2 * k + layers : 2 * k + 2 * layers]
    numbers = stats[2 * k + 2 * layers]
    weight_squares, bias_step_squares, bias_squares = numbers[: 3 * k].reshape(3, layers, 5)
    row_total = numbers[3 * k : 3 * k + layers]
    out_squares = numbers[3 * k + layers : 3 * k + 2 * layers]

    new_in_rows = DECAY * in_rows + (1.0 - DECAY) * row_sum / sizes[None, :, None]
    row_mean = jnp.mean(new_in_rows, axis=2)
    step_squares = row_mean * jnp.sum(row_step / new_in_rows, axis=2)
    factor_in = shrink_factor(step_squares, weight_squares, features * sizes[None, :])
    own_rows = jnp.sum(new_in_rows * here[None, :, None], axis=1)
    own_mean = jnp.sum(row_mean * here, axis=1)
    own_factor = jnp.sum(factor_in * here, axis=1)
    step_in = grad_in * lax.rsqrt(
        own_rows[:, None, :] * new_in_cols[:, :, None] / own_mean[:, None, None]
    )
    new_in_proj = jnp.swapaxes(w_own - own_factor[:, None, None] * step_in, 1, 2)

    new_out_cols = DECAY * out_cols + (1.0 - DECAY) * col_sum / FF
    out_mean = row_total / FF
    factor_out = shrink_factor(
        out_mean * jnp.sum(col_step / new_out_cols, axis=1), out_squares, float(FF * features)
    )
    own_cols = jnp.sum(layer_here[:, None] * new_out_cols, axis=0)
    step_out = grad_out * lax.rsqrt(
        new_out_rows[:, None] * own_cols[None, :] / jnp.sum(layer_here * out_mean)
    )
    new_out_proj = out_proj - jnp.sum(layer_here * factor_out) * step_out
    factor_bias = shrink_factor(bias_step_squares, bias_squares, sizes[None, :])
    new_in_bias = in_bias - jnp.sum(factor_bias * here, axis=1)[:, None] * bias_step

    new_vector_moment = DECAY * vector_moment + (1.0 - DECAY) * grad_vec * grad_vec
    vector_step = grad_vec * lax.rsqrt(new_vector_moment)
    factor_vec = shrink_factor(
        jnp.sum(vector_step * vector_step, axis=1),
        jnp.sum(vectors * vectors, axis=1),
        float(features),
    )
    new_vectors = vectors - factor_vec[:, None] * vector_step
    square_table = grad_table * grad_table
    new_embed_rows = DECAY * embed_rows + (1.0 - DECAY) * jnp.mean(square_table, axis=1)
    new_embed_cols = DECAY * embed_cols + (1.0 - DECAY) * jnp.mean(square_table, axis=0)
    table_step = grad_table * lax.rsqrt(
        new_embed_rows[:, None] * new_embed_cols[None, :] / jnp.mean(new_embed_rows)
    )
    factor_table = shrink_factor(
        jnp.sum(table_step * table_step),
        jnp.sum(embedding * embedding),
        float(vocab * features),
    )
    new_embedding = embedding - factor_table * table_step
    return (
        loss,
        new_in_proj,
        new_in_bias,
        new_out_proj,
        new_vectors,
        new_embedding,
        new_in_rows,
        new_in_cols,
        new_out_rows,
        new_out_cols,
        new_bias_moment,
        new_vector_moment,
        new_embed_rows,
        new_embed_cols,
    )


def solution(mesh):
    both = AXES
    return jax.shard_map(
        functools.partial(local, mesh.shape["dp"] * mesh.shape["fsdp"]),
        mesh=mesh,
        in_specs=(
            P(None, both, None),
            P(None, both, None),
            P(None, both),
            P(None, both, None),
            P(None, None, both),
            P(None, both),
            P(both, None),
            P(),
            P(),
            P(),
            P(None, both),
            P(both),
            P(),
            P(None, both),
            P(),
            P(),
            P(),
        ),
        out_specs=(
            P(),
            P(None, None, both),
            P(None, both),
            P(both, None),
            P(),
            P(),
            P(),
            P(None, both),
            P(both),
            P(),
            P(None, both),
            P(),
            P(),
            P(),
        ),
        check_vma=False,
    )
```
